256 devices in a mesh: span: 8 (over z), xsec: 8 (over x, core), leaf: 4 (over y).
Axes of the slice: x: 4, y: 4, z: 8, core: 2. Of those that a mesh axis runs over, the one named last changes fastest.
Arguments:
- snapshots: float32 [3, 65536, 256], P(None, ('span', 'xsec', 'leaf')), may hold values from -1800 to 1800
- member_ends: int32 [2, 262144], P(None, ('span', 'xsec', 'leaf')), may hold values from 0 to 383, as said below
- member_dir: float32 [3, 262144], P(None, ('span', 'xsec', 'leaf')), may hold values from -3 to 3
- member_stiff: float32 [262144], P(('span', 'xsec', 'leaf')), may hold values from 0.25 to 24
Outputs:
- basis: float32 [3, 65536, 256], P(None, ('span', 'xsec', 'leaf'))
- forces: float32 [3, 65536, 256], P(None, ('span', 'xsec', 'leaf'))
- reduced: float32 [256, 256], replicated
- coef: float32 [256, 256], replicated
- column_energy: float32 [256], replicated
The draws below stay inside these ranges and needn't reach their ends.
Inputs may be any that keep to these rules, and one draw needn't show every extreme that they name: member_ends[0] names a node of the member's own device block; member_ends[1] names such a node or, from 256 on, a node of the top level of the slab directly below in the same sector; both ends of a member lie on the same or neighbouring levels.
All inputs are finite; a program needn't handle non-finite values.
Results may differ from the reference program's by a relative error of at most 0.0008.
Values sent between devices are 32-bit elements; how exact they have to be, the bound alone decides.
A program may use at most 64 MiB of HBM per device.

```python
import math
import jax
import jax.numpy as jnp
from jax import lax

K = 256
LEV_DEV = 2
SEC_NODES = 128
NODE_DEV = 256
MEMB_DEV = 1024
SECTORS = 32
NODES = 65536
MEMBERS = 262144
N_SPAN = 8
N_XSEC = 8
N_LEAF = 4


def draw_snapshots(key, part):
    key_noise = jax.random.fold_in(key, 11)
    key_common = jax.random.fold_in(key, 12)
    key_column = jax.random.fold_in(key, 13)
    key_row = jax.random.fold_in(key, 14)
    key_weak = jax.random.fold_in(key, 15)
    ratio = min(8.0, 3.0 * NODE_DEV / K)
    weakest = 0.002 * 8.0 / ratio
    noise = jnp.clip(jax.random.normal(key_noise, (3, NODES, K), jnp.float32), -5.0, 5.0)
    common = jnp.clip(jax.random.normal(key_common, (3, NODES, 1), jnp.float32), -4.0, 4.0)
    row_span = math.log(10.0)
    weight = jnp.exp(jax.random.uniform(key_weak, (K,), jnp.float32, math.log(weakest), 0.0))
    column_scale = jnp.exp(jax.random.uniform(key_column, (K,), jnp.float32, 0.0, math.log(10.0)))
    row_scale = jnp.exp(jax.random.uniform(key_row, (3, NODES, 1), jnp.float32, 0.0, row_span))
    height = 1.0 + 2.0 * jnp.arange(NODES, dtype=jnp.float32) / NODES
    mixed = common + weight[None, None, :] * noise
    values = mixed * column_scale[None, None, :] * row_scale * height[None, :, None]
    return jnp.clip(values, -1800.0, 1800.0)


def draw_member_ends(key, part):
    key_first = jax.random.fold_in(key, 21)
    key_kind = jax.random.fold_in(key, 22)
    key_across = jax.random.fold_in(key, 23)
    key_down = jax.random.fold_in(key, 24)
    first_end = jax.random.randint(key_first, (MEMBERS,), 0, NODE_DEV, dtype=jnp.int32)
    level_index = first_end // SEC_NODES
    position = first_end % SEC_NODES
    member_kind = jax.random.randint(key_kind, (MEMBERS,), 0, 3, dtype=jnp.int32)
    across_step = jax.random.randint(key_across, (MEMBERS,), 1, 4, dtype=jnp.int32)
    down_step = jax.random.randint(key_down, (MEMBERS,), -2, 3, dtype=jnp.int32)
    across_end = level_index * SEC_NODES + (position + across_step) % SEC_NODES
    down_position = (position + down_step) % SEC_NODES
    down_end = jnp.where(level_index > 0, (level_index - 1) * SEC_NODES + down_position, NODE_DEV + down_position)
    second_end = jnp.where(member_kind == 0, across_end, down_end)
    return jnp.stack([first_end, second_end]).astype(jnp.int32)


def draw_member_stiff(key, part):
    key_base = jax.random.fold_in(key, 31)
    lowest, highest_value = (0.5, 4.0)
    base = jnp.exp(jax.random.uniform(key_base, (MEMBERS,), jnp.float32, math.log(lowest), math.log(highest_value)))
    height = jnp.arange(MEMBERS, dtype=jnp.float32) / MEMBERS
    return base * (3.0 - 2.0 * height)


def level_of(stream_key, shape, pieces, smallest, high):
    factor_of, own = 1.0, jax.random.fold_in(stream_key, 6)
    for dim, parts in pieces:
        steps = jnp.exp(jax.random.uniform(jax.random.fold_in(own, dim), (parts,), jnp.float32, smallest / len(pieces), high / len(pieces)))
        factor_of = factor_of * jnp.repeat(steps, shape[dim] // parts).reshape([-1 if axis == dim else 1 for axis in range(len(shape))])
    return factor_of


def gaussian(key, dims, scale, bound, split=(), kind=jnp.bfloat16):
    level = level_of(key, dims, split, -0.22, 0.18) if split else 1.0
    values = jax.random.normal(key, dims, jnp.float32) * scale * level
    return jnp.minimum(jnp.maximum(values, -bound), bound).astype(kind)


def setup_inputs(seed: int = 0) -> dict:
    key_of = jax.random.split(jax.random.key(seed), 5)
    return {
        "snapshots": draw_snapshots(jax.random.fold_in(key_of[4], 71), 0),
        "member_ends": draw_member_ends(jax.random.fold_in(key_of[4], 71), 0),
        "member_dir": gaussian(key_of[2], (3, MEMBERS), 0.5, 3.0, ((1, 256),), jnp.float32),
        "member_stiff": draw_member_stiff(jax.random.fold_in(key_of[4], 71), 0),
    }


def member_block(basis, member_ends, member_dir, member_stiff, device_index):
    start = (device_index * MEMB_DEV).astype(jnp.int32)
    ends_here = lax.dynamic_slice_in_dim(member_ends, start, MEMB_DEV, 1)
    direction = lax.dynamic_slice_in_dim(member_dir, start, MEMB_DEV, 1)
    stiffness = lax.dynamic_slice_in_dim(member_stiff, start, MEMB_DEV, 0)
    own_block = lax.dynamic_slice_in_dim(basis, (device_index * NODE_DEV).astype(jnp.int32), NODE_DEV, 1)
    lower_index = jnp.maximum(device_index - SECTORS, 0)
    top_start = (lower_index * NODE_DEV + (LEV_DEV - 1) * SEC_NODES).astype(jnp.int32)
    below_top = lax.dynamic_slice_in_dim(basis, top_start, SEC_NODES, 1)
    below_top = jnp.where(device_index >= SECTORS, below_top, jnp.zeros_like(below_top))
    extended = jnp.concatenate([own_block, below_top], axis=1)
    first_end = ends_here[0]
    second_end = ends_here[1]
    difference = extended[:, first_end, :] - extended[:, second_end, :]
    elongation = jnp.einsum('cm,cmk->mk', direction, difference, precision=lax.Precision.HIGHEST)
    axial_force = elongation * stiffness[:, None]
    nodal_push = direction[:, :, None] * axial_force[None, :, :]
    extended_forces = jnp.zeros_like(extended).at[:, first_end, :].add(nodal_push).at[:, second_end, :].add(-nodal_push)
    partial_sum = jnp.einsum('mk,ml->kl', elongation, axial_force, precision=lax.Precision.HIGHEST)
    return (extended_forces, partial_sum)

def reference(snapshots, member_ends, member_dir, member_stiff):
    flattened = snapshots.reshape(3 * NODES, K)
    column_energy = jnp.log(lax.optimization_barrier(jnp.sum(flattened * flattened, axis=0)) / (3 * NODES))
    factor_q, factor_r = jnp.linalg.qr(flattened)
    signs = jnp.sign(jnp.diagonal(factor_r))
    root_rows = jnp.sqrt(jnp.float32(3 * NODES))
    basis = (factor_q * signs[None, :] * root_rows).reshape(3, NODES, K)
    coef = factor_r * signs[:, None] / root_rows
    device_count = N_SPAN * N_XSEC * N_LEAF
    indices = jnp.arange(device_count, dtype=jnp.int32)
    extended_forces, partials = lax.map(lambda index: member_block(basis, member_ends, member_dir, member_stiff, index), indices)
    own_forces = extended_forces[:, :, :NODE_DEV, :]
    returned = extended_forces[:, :, NODE_DEV:, :]
    from_above = jnp.concatenate([returned[SECTORS:], jnp.zeros_like(returned[:SECTORS])], axis=0)
    own_forces = own_forces.at[:, :, NODE_DEV - SEC_NODES:, :].add(from_above)
    forces = own_forces.transpose(1, 0, 2, 3).reshape(3, NODES, K)
    reduced = lax.optimization_barrier(jnp.sum(partials, axis=0)) / (3 * NODES)
    return (basis, forces, reduced, coef, column_energy)
```

```python
import functools
import math

import jax
import jax.numpy as jnp
from jax import lax
from jax.experimental import pallas as pl
from jax.experimental.pallas import tpu as pltpu
from jax.sharding import Mesh
from jax.sharding import PartitionSpec as P

SEC_NODES = 128
XSEC = ("xsec_0", "xsec_1")
SPAN_XSEC_LEAF = ("span", "xsec_0", "xsec_1", "leaf")
TILE = 8
LANES = 128
CHUNK = 256

highest = lax.Precision.HIGHEST
f32 = jnp.float32


def shifted(array, axis, by):
    length = lax.axis_size(axis)
    pairs = [(i, i + by) for i in range(length) if 0 <= i + by < length]
    return lax.ppermute(array, axis, pairs)


def cut_along(array, dim, length):
    shape = array.shape
    blocks = array.reshape(*shape[:dim], length, shape[dim] // length, *shape[dim + 1 :])
    return jnp.moveaxis(blocks, dim, 0)


def sent_and_summed(array, axis, dim):
    length = lax.axis_size(axis)
    blocks = lax.all_to_all(cut_along(array, dim, length), axis, 0, 0, tiled=True)
    return jnp.sum(blocks, axis=0)


def sum_in_two_steps(array, axes, dim):
    far, near = axes
    blocks = cut_along(array, dim, lax.axis_size(far))
    nearer = sent_and_summed(blocks, near, dim + 1)
    arrived = lax.all_to_all(nearer, far, split_axis=0, concat_axis=0, tiled=True)
    return arrived.sum(axis=0)


def from_everyone(array, axis):
    length = lax.axis_size(axis)
    return lax.all_to_all(
        jnp.broadcast_to(array[None], (length, *array.shape)), axis, 0, 0, tiled=True
    )


def whole_of(array, axes):
    far, near = axes
    blocks = from_everyone(from_everyone(array, far), near)
    return blocks.swapaxes(0, 1).reshape(-1, *array.shape[1:])


def sum_by_parts(lines, axes):
    return whole_of(sum_in_two_steps(lines, axes, 0), axes)


def dot_f32(a, b, over_a=1, over_b=0):
    return lax.dot_general(
        a, b, (((over_a,), (over_b,)), ((), ())), precision=highest, preferred_element_type=f32
    )


def dot_bf16(a, b):
    return jnp.dot(a, b, preferred_element_type=f32)


def in_three(x):
    high = x.astype(jnp.bfloat16)
    rest = x - high.astype(f32)
    middle = rest.astype(jnp.bfloat16)
    return high, middle, (rest - middle.astype(f32)).astype(jnp.bfloat16)


def over_lanes(column):
    return jnp.broadcast_to(column, (TILE, LANES))


def over_rows(row):
    return jnp.broadcast_to(row, (TILE, LANES))


def factor_block(block):
    count = LANES // TILE
    lane = lax.broadcasted_iota(jnp.int32, (TILE, LANES), 1)
    sub = lax.broadcasted_iota(jnp.int32, (TILE, LANES), 0)
    left = [block[TILE * i : TILE * i + TILE, :] for i in range(count)]
    right = [jnp.where(lane == sub + TILE * i, 1.0, 0.0).astype(f32) for i in range(count)]
    for k in range(count):
        own_left, own_right = left[k], right[k]
        at = TILE * k
        columns = [over_lanes(own_left[:, at + j : at + j + 1]) for j in range(TILE)]
        pivot_left, pivot_right, pivot_columns, inverse = [], [], [], []
        scale = jnp.zeros((TILE, LANES), f32)
        for j in range(TILE):
            pivot = over_rows(columns[j][j : j + 1, :])
            inverse.append(1.0 / pivot)
            pivot_left.append(over_rows(own_left[j : j + 1, :]))
            pivot_right.append(over_rows(own_right[j : j + 1, :]))
            pivot_columns.append([over_rows(columns[l][j : j + 1, :]) for l in range(TILE)])
            factor = jnp.where(sub > j, columns[j] * inverse[j], 0.0)
            for l in range(j + 1, TILE):
                columns[l] = columns[l] - factor * pivot_columns[j][l]
            own_left = own_left - factor * pivot_left[j]
            own_right = own_right - factor * pivot_right[j]
            scale = jnp.where(sub == j, lax.rsqrt(pivot), scale)
        for i in range(k + 1, count):
            columns = [over_lanes(left[i][:, at + j : at + j + 1]) for j in range(TILE)]
            row_left, row_right = left[i], right[i]
            for j in range(TILE):
                factor = columns[j] * inverse[j]
                for l in range(j + 1, TILE):
                    columns[l] = columns[l] - factor * pivot_columns[j][l]
                row_left = row_left - factor * pivot_left[j]
                row_right = row_right - factor * pivot_right[j]
            left[i], right[i] = row_left, row_right
        left[k] = jnp.where(lane >= sub + at, own_left * scale, 0.0)
        right[k] = own_right * scale
    return jnp.concatenate(left, 0), jnp.concatenate(right, 0)


def factor_into(gram_ref, upper_ref, inverse_ref):
    upper_a, lower_a = factor_block(gram_ref[:LANES, :LANES])
    across = dot_f32(lower_a, gram_ref[:LANES, LANES:])
    upper_b, lower_b = factor_block(gram_ref[LANES:, LANES:] - dot_f32(across, across, 0, 0))
    zero = jnp.zeros((LANES, LANES), f32)
    upper_ref[:LANES, :LANES] = upper_a
    upper_ref[:LANES, LANES:] = across
    upper_ref[LANES:, :LANES] = zero
    upper_ref[LANES:, LANES:] = upper_b
    inverse_a, inverse_b = lower_a.T, lower_b.T
    inverse_ref[:LANES, :LANES] = inverse_a
    inverse_ref[:LANES, LANES:] = -dot_f32(inverse_a, dot_f32(across, inverse_b))
    inverse_ref[LANES:, :LANES] = zero
    inverse_ref[LANES:, LANES:] = inverse_b


def members_kernel(field, below, ends, direction, stiff, elongation, forces, parts):
    components, own, width = field.shape
    nodes = own + below.shape[1]
    members = ends.shape[1]
    for c in range(components):
        for start, ref in ((0, field), (own, below)):
            for p, part in enumerate(in_three(ref[c])):
                parts[p, c, start : start + ref.shape[1], :] = part
    table = jnp.concatenate(
        [direction[...], stiff[...], ends[...].astype(f32), jnp.zeros((2, members), f32)], 0
    ).T
    forces[...] = jnp.zeros_like(forces)
    for start in range(0, members, CHUNK):
        rows = slice(start, start + CHUNK)
        of = [table[rows, i : i + 1] for i in range(6)]
        node = lax.broadcasted_iota(jnp.int32, (CHUNK, nodes), 1).astype(f32)
        pick = jnp.where(node == of[4], 1.0, 0.0) - jnp.where(node == of[5], 1.0, 0.0)
        pick = pick.astype(jnp.bfloat16)
        node = lax.broadcasted_iota(jnp.int32, (nodes, CHUNK), 0)
        spread = jnp.where(node == ends[0:1, rows], 1.0, 0.0)
        spread = spread - jnp.where(node == ends[1:2, rows], 1.0, 0.0)
        spread = spread.astype(jnp.bfloat16)
        stretch = jnp.zeros((CHUNK, width), f32)
        for c in range(components):
            difference = dot_bf16(pick, parts[2, c])
            difference = difference + dot_bf16(pick, parts[1, c])
            difference = difference + dot_bf16(pick, parts[0, c])
            stretch = stretch + of[c] * difference
        elongation[rows, :] = stretch
        pull = stretch * of[3]
        for c in range(components):
            high, middle, low = in_three(of[c] * pull)
            push = dot_bf16(spread, low) + dot_bf16(spread, middle) + dot_bf16(spread, high)
            forces[c] = forces[c] + push


def member_forces(field, below, ends, direction, stiff):
    components, own, width = field.shape
    nodes, members = own + below.shape[1], ends.shape[1]
    return pl.pallas_call(
        members_kernel,
        out_shape=(
            jax.ShapeDtypeStruct((members, width), f32),
            jax.ShapeDtypeStruct((components, nodes, width), f32),
        ),
        scratch_shapes=[pltpu.VMEM((3, components, nodes, width), jnp.bfloat16)],
        compiler_params=pltpu.CompilerParams(vmem_limit_bytes=60 << 20),
        cost_estimate=pl.CostEstimate(
            flops=12 * components * nodes * members * width, bytes_accessed=4 << 20, transcendentals=0
        ),
        name="member_forces",
    )(field, below, ends, direction, stiff.reshape(1, -1))


def first_kernel(gram, field, elongation, stiff, upper, inverse, first, sums):
    factor_into(gram, upper, inverse)
    transform = inverse[...]
    width = transform.shape[0]
    first[...] = dot_f32(field[...], transform)
    sums[:width, :] = dot_f32(first[...], first[...], 0, 0)
    stretch = dot_f32(elongation[...], transform)
    sums[width:, :] = dot_f32(stretch, stretch * stiff[...].T[:, :1], 0, 0)


def first_pass(gram, flattened, elongation, stiff):
    rows, width = flattened.shape
    square = jax.ShapeDtypeStruct((width, width), f32)
    stiff = jnp.broadcast_to(stiff.reshape(1, -1), (TILE, stiff.shape[0]))
    return pl.pallas_call(
        first_kernel,
        out_shape=(
            square,
            square,
            jax.ShapeDtypeStruct((rows, width), f32),
            jax.ShapeDtypeStruct((2 * width, width), f32),
        ),
        compiler_params=pltpu.CompilerParams(vmem_limit_bytes=60 << 20),
        name="first_pass",
    )(gram, flattened, elongation, stiff)


def second_kernel(
    total_rows, own, sums, upper_first, inverse_first, first, raw, returned, basis, forces, reduced,
    coef, upper, inverse,
):
    width = inverse.shape[0]
    root = math.sqrt(total_rows)
    factor_into(sums.at[:width, :], upper, inverse)
    transform = inverse[...]
    basis[...] = dot_f32(first[...], transform) * root
    both = dot_f32(inverse_first[...], transform) * root
    for c in range(raw.shape[0]):
        low = own - returned.shape[1]
        forces[c, :low, :] = dot_f32(raw[c, :low, :], both)
        forces[c, low:, :] = dot_f32(raw[c, low:own, :] + returned[c], both)
    reduced[...] = dot_f32(transform, dot_f32(sums[width:, :], transform), 0, 0)
    coef[...] = dot_f32(upper[...], upper_first[...]) * (1.0 / root)


def second_pass(sums, upper, inverse, first, raw, returned, total_rows):
    components, _, width = raw.shape
    own = first.shape[0] // components
    square = jax.ShapeDtypeStruct((width, width), f32)
    return pl.pallas_call(
        functools.partial(second_kernel, total_rows, own),
        out_shape=(
            jax.ShapeDtypeStruct(first.shape, f32),
            jax.ShapeDtypeStruct((components, own, width), f32),
            square,
            square,
        ),
        scratch_shapes=[pltpu.VMEM((width, width), f32)] * 2,
        compiler_params=pltpu.CompilerParams(vmem_limit_bytes=60 << 20),
        name="second_pass",
    )(sums, upper, inverse, first, raw, returned)


def local(snapshots, member_ends, member_dir, member_stiff):
    components, node_count, width = snapshots.shape
    flattened = snapshots.reshape(components * node_count, width)
    devices_all = lax.axis_size("span") * lax.axis_size(XSEC) * lax.axis_size("leaf")
    total_rows = components * node_count * devices_all
    axes = (("span", "xsec_0"), ("xsec_1", "leaf"))
    below = shifted(snapshots[:, node_count - SEC_NODES :, :], "span", 1)
    gram = sum_by_parts(dot_f32(flattened, flattened, 0, 0), axes)
    column_energy = jnp.log(jnp.diagonal(gram) / total_rows)
    elongation, raw = member_forces(snapshots, below, member_ends, member_dir, member_stiff)
    returned = shifted(raw[:, node_count:, :], "span", -1)
    upper, inverse, first, sums = first_pass(gram, flattened, elongation, member_stiff)
    sums = sum_by_parts(sums, axes)
    basis, forces, reduced, coef = second_pass(
        sums, upper, inverse, first, raw, returned, total_rows
    )
    return (basis.reshape(snapshots.shape), forces, reduced, coef, column_energy)


def solution(mesh):
    torus = Mesh(
        mesh.devices.reshape(mesh.shape["span"], 4, 2, mesh.shape["leaf"]),
        ("span", "xsec_0", "xsec_1", "leaf"),
    )
    return jax.shard_map(
        local,
        mesh=torus,
        in_specs=(
            P(None, SPAN_XSEC_LEAF, None),
            P(None, SPAN_XSEC_LEAF),
            P(None, SPAN_XSEC_LEAF),
            P(SPAN_XSEC_LEAF),
        ),
        out_specs=(P(None, SPAN_XSEC_LEAF, None), P(None, SPAN_XSEC_LEAF, None), P(), P(), P()),
        check_vma=False,
    )
```

```python
import functools
import math

import jax
import jax.numpy as jnp
from jax import lax
from jax.experimental import pallas as pl
from jax.experimental.pallas import tpu as pltpu
from jax.sharding import PartitionSpec as P

SEC_NODES = 128
SPAN_XSEC_LEAF = ("span", "xsec", "leaf")
TILE = 8
LANES = 128
CHUNK = 256

highest = lax.Precision.HIGHEST
f32 = jnp.float32


def shifted(array, axis, by):
    length = lax.axis_size(axis)
    pairs = [(i, i + by) for i in range(length) if 0 <= i + by < length]
    return lax.ppermute(array, axis, pairs)


def all_sum_kernel(part, total, arrived, planes, gathered, sent, got):
    near, far = part.shape[0], planes.shape[0]
    leaves = lax.axis_size("leaf")
    chips = near // (2 * leaves)
    span, xsec, leaf = (lax.axis_index(name) for name in ("span", "xsec", "leaf"))
    chip, core = xsec // 2, xsec % 2
    own = xsec * leaves + leaf

    def place(step):
        there = (chip + (step // 2) % chips) % chips
        return there * 2 + (core + step % 2) % 2, (leaf + step // (2 * chips)) % leaves

    def in_slab(step):
        other, side = place(step)
        return {"xsec": other, "leaf": side}

    def over_slabs(step):
        return {"span": (span + step) % far}

    def scatter(step):
        other, side = place(step)
        return pltpu.make_async_remote_copy(
            part.at[other * leaves + side], arrived.at[step], sent.at[0, step], got.at[0, step],
            in_slab(step),
        )

    def exchange(step):
        return pltpu.make_async_remote_copy(
            planes.at[span], planes.at[span], sent.at[1, step], got.at[1, step], over_slabs(step)
        )

    def gather(step):
        return pltpu.make_async_remote_copy(
            gathered.at[own], gathered.at[own], sent.at[2, step], got.at[2, step], in_slab(step)
        )

    def each(count, act):
        lax.fori_loop(1, count, lambda step, _: (act(step), 0)[1], 0)

    barrier = pltpu.get_barrier_semaphore()
    each(near, lambda step: pl.semaphore_signal(barrier, inc=1, device_id=in_slab(step)))
    each(far, lambda step: pl.semaphore_signal(barrier, inc=1, device_id=over_slabs(step)))
    pl.semaphore_wait(barrier, near + far - 2)
    each(near, lambda step: scatter(step).start())
    each(near, lambda step: scatter(step).wait_recv())
    block = part[own]
    for step in range(1, near):
        block = block + arrived[step]
    planes[span] = block
    each(far, lambda step: exchange(step).start())
    each(far, lambda step: exchange(step).wait_recv())
    block = planes[0]
    for other in range(1, far):
        block = block + planes[other]
    gathered[own] = block
    each(near, lambda step: gather(step).start())
    each(near, lambda step: gather(step).wait_recv())
    total[...] = gathered[...]
    each(near, lambda step: scatter(step).wait_send())
    each(far, lambda step: exchange(step).wait_send())
    each(near, lambda step: gather(step).wait_send())


def all_sum(blocks, key):
    near, lines, lanes = blocks.shape
    far = lax.axis_size("span")
    return pl.pallas_call(
        all_sum_kernel,
        out_shape=jax.ShapeDtypeStruct(blocks.shape, f32),
        scratch_shapes=[
            pltpu.VMEM(blocks.shape, f32),
            pltpu.VMEM((far, lines, lanes), f32),
            pltpu.VMEM(blocks.shape, f32),
            pltpu.SemaphoreType.DMA((3, near)),
            pltpu.SemaphoreType.DMA((3, near)),
        ],
        compiler_params=pltpu.CompilerParams(collective_id=key, has_side_effects=True),
        name="all_sum",
    )(blocks)


def dot_f32(a, b, over_a=1, over_b=0):
    return lax.dot_general(
        a, b, (((over_a,), (over_b,)), ((), ())), precision=highest, preferred_element_type=f32
    )


def dot_bf16(a, b):
    return jnp.dot(a, b, preferred_element_type=f32)


def in_three(x):
    high = x.astype(jnp.bfloat16)
    rest = x - high.astype(f32)
    middle = rest.astype(jnp.bfloat16)
    return high, middle, (rest - middle.astype(f32)).astype(jnp.bfloat16)


def over_lanes(column):
    return jnp.broadcast_to(column, (TILE, LANES))


def over_rows(row):
    return jnp.broadcast_to(row, (TILE, LANES))


def factor_block(block):
    count = LANES // TILE
    lane = lax.broadcasted_iota(jnp.int32, (TILE, LANES), 1)
    sub = lax.broadcasted_iota(jnp.int32, (TILE, LANES), 0)
    left = [block[TILE * i : TILE * i + TILE, :] for i in range(count)]
    right = [jnp.where(lane == sub + TILE * i, 1.0, 0.0).astype(f32) for i in range(count)]
    for k in range(count):
        own_left, own_right = left[k], right[k]
        at = TILE * k
        columns = [over_lanes(own_left[:, at + j : at + j + 1]) for j in range(TILE)]
        pivot_left, pivot_right, pivot_columns, inverse = [], [], [], []
        scale = jnp.zeros((TILE, LANES), f32)
        for j in range(TILE):
            pivot = over_rows(columns[j][j : j + 1, :])
            inverse.append(1.0 / pivot)
            pivot_left.append(over_rows(own_left[j : j + 1, :]))
            pivot_right.append(over_rows(own_right[j : j + 1, :]))
            pivot_columns.append([over_rows(columns[l][j : j + 1, :]) for l in range(TILE)])
            factor = jnp.where(sub > j, columns[j] * inverse[j], 0.0)
            for l in range(j + 1, TILE):
                columns[l] = columns[l] - factor * pivot_columns[j][l]
            own_left = own_left - factor * pivot_left[j]
            own_right = own_right - factor * pivot_right[j]
            scale = jnp.where(sub == j, lax.rsqrt(pivot), scale)
        for i in range(k + 1, count):
            columns = [over_lanes(left[i][:, at + j : at + j + 1]) for j in range(TILE)]
            row_left, row_right = left[i], right[i]
            for j in range(TILE):
                factor = columns[j] * inverse[j]
                for l in range(j + 1, TILE):
                    columns[l] = columns[l] - factor * pivot_columns[j][l]
                row_left = row_left - factor * pivot_left[j]
                row_right = row_right - factor * pivot_right[j]
            left[i], right[i] = row_left, row_right
        left[k] = jnp.where(lane >= sub + at, own_left * scale, 0.0)
        right[k] = own_right * scale
    return jnp.concatenate(left, 0), jnp.concatenate(right, 0)


def factor_into(gram_ref, upper_ref, inverse_ref):
    upper_a, lower_a = factor_block(gram_ref[:LANES, :LANES])
    across = dot_f32(lower_a, gram_ref[:LANES, LANES:])
    upper_b, lower_b = factor_block(gram_ref[LANES:, LANES:] - dot_f32(across, across, 0, 0))
    zero = jnp.zeros((LANES, LANES), f32)
    upper_ref[:LANES, :LANES] = upper_a
    upper_ref[:LANES, LANES:] = across
    upper_ref[LANES:, :LANES] = zero
    upper_ref[LANES:, LANES:] = upper_b
    inverse_a, inverse_b = lower_a.T, lower_b.T
    inverse_ref[:LANES, :LANES] = inverse_a
    inverse_ref[:LANES, LANES:] = -dot_f32(inverse_a, dot_f32(across, inverse_b))
    inverse_ref[LANES:, :LANES] = zero
    inverse_ref[LANES:, LANES:] = inverse_b


def members_kernel(field, below, ends, direction, stiff, elongation, forces, parts):
    components, own, width = field.shape
    nodes = own + below.shape[1]
    members = ends.shape[1]
    for c in range(components):
        for start, ref in ((0, field), (own, below)):
            for p, part in enumerate(in_three(ref[c])):
                parts[p, c, start : start + ref.shape[1], :] = part
    table = jnp.concatenate(
        [direction[...], stiff[...], ends[...].astype(f32), jnp.zeros((2, members), f32)], 0
    ).T
    forces[...] = jnp.zeros_like(forces)
    for start in range(0, members, CHUNK):
        rows = slice(start, start + CHUNK)
        of = [table[rows, i : i + 1] for i in range(6)]
        node = lax.broadcasted_iota(jnp.int32, (CHUNK, nodes), 1).astype(f32)
        pick = jnp.where(node == of[4], 1.0, 0.0) - jnp.where(node == of[5], 1.0, 0.0)
        pick = pick.astype(jnp.bfloat16)
        node = lax.broadcasted_iota(jnp.int32, (nodes, CHUNK), 0)
        spread = jnp.where(node == ends[0:1, rows], 1.0, 0.0)
        spread = spread - jnp.where(node == ends[1:2, rows], 1.0, 0.0)
        spread = spread.astype(jnp.bfloat16)
        stretch = jnp.zeros((CHUNK, width), f32)
        for c in range(components):
            difference = dot_bf16(pick, parts[2, c])
            difference = difference + dot_bf16(pick, parts[1, c])
            difference = difference + dot_bf16(pick, parts[0, c])
            stretch = stretch + of[c] * difference
        elongation[rows, :] = stretch
        pull = stretch * of[3]
        for c in range(components):
            high, middle, low = in_three(of[c] * pull)
            push = dot_bf16(spread, low) + dot_bf16(spread, middle) + dot_bf16(spread, high)
            forces[c] = forces[c] + push


def member_forces(field, below, ends, direction, stiff):
    components, own, width = field.shape
    nodes, members = own + below.shape[1], ends.shape[1]
    return pl.pallas_call(
        members_kernel,
        out_shape=(
            jax.ShapeDtypeStruct((members, width), f32),
            jax.ShapeDtypeStruct((components, nodes, width), f32),
        ),
        scratch_shapes=[pltpu.VMEM((3, components, nodes, width), jnp.bfloat16)],
        compiler_params=pltpu.CompilerParams(vmem_limit_bytes=60 << 20),
        cost_estimate=pl.CostEstimate(
            flops=12 * components * nodes * members * width, bytes_accessed=4 << 20, transcendentals=0
        ),
        name="member_forces",
    )(field, below, ends, direction, stiff.reshape(1, -1))


def first_kernel(gram, field, elongation, stiff, upper, inverse, first, sums):
    factor_into(gram, upper, inverse)
    transform = inverse[...]
    width = transform.shape[0]
    first[...] = dot_f32(field[...], transform)
    sums[:width, :] = dot_f32(first[...], first[...], 0, 0)
    stretch = dot_f32(elongation[...], transform)
    sums[width:, :] = dot_f32(stretch, stretch * stiff[...].T[:, :1], 0, 0)


def first_pass(gram, flattened, elongation, stiff):
    rows, width = flattened.shape
    square = jax.ShapeDtypeStruct((width, width), f32)
    stiff = jnp.broadcast_to(stiff.reshape(1, -1), (TILE, stiff.shape[0]))
    return pl.pallas_call(
        first_kernel,
        out_shape=(
            square,
            square,
            jax.ShapeDtypeStruct((rows, width), f32),
            jax.ShapeDtypeStruct((2 * width, width), f32),
        ),
        compiler_params=pltpu.CompilerParams(vmem_limit_bytes=60 << 20),
        name="first_pass",
    )(gram, flattened, elongation, stiff)


def second_kernel(
    total_rows, own, sums, upper_first, inverse_first, first, raw, returned, basis, forces, reduced,
    coef, upper, inverse,
):
    width = inverse.shape[0]
    root = math.sqrt(total_rows)
    factor_into(sums.at[:width, :], upper, inverse)
    transform = inverse[...]
    basis[...] = dot_f32(first[...], transform) * root
    both = dot_f32(inverse_first[...], transform) * root
    for c in range(raw.shape[0]):
        low = own - returned.shape[1]
        forces[c, :low, :] = dot_f32(raw[c, :low, :], both)
        forces[c, low:, :] = dot_f32(raw[c, low:own, :] + returned[c], both)
    reduced[...] = dot_f32(transform, dot_f32(sums[width:, :], transform), 0, 0)
    coef[...] = dot_f32(upper[...], upper_first[...]) * (1.0 / root)


def second_pass(sums, upper, inverse, first, raw, returned, total_rows):
    components, _, width = raw.shape
    own = first.shape[0] // components
    square = jax.ShapeDtypeStruct((width, width), f32)
    return pl.pallas_call(
        functools.partial(second_kernel, total_rows, own),
        out_shape=(
            jax.ShapeDtypeStruct(first.shape, f32),
            jax.ShapeDtypeStruct((components, own, width), f32),
            square,
            square,
        ),
        scratch_shapes=[pltpu.VMEM((width, width), f32)] * 2,
        compiler_params=pltpu.CompilerParams(vmem_limit_bytes=60 << 20),
        name="second_pass",
    )(sums, upper, inverse, first, raw, returned)


def local(snapshots, member_ends, member_dir, member_stiff):
    components, node_count, width = snapshots.shape
    flattened = snapshots.reshape(components * node_count, width)
    devices_all = lax.axis_size("span") * lax.axis_size("xsec") * lax.axis_size("leaf")
    total_rows = components * node_count * devices_all
    below = shifted(snapshots[:, node_count - SEC_NODES :, :], "span", 1)
    near = lax.axis_size("xsec") * lax.axis_size("leaf")
    gram = dot_f32(flattened, flattened, 0, 0)
    gram = all_sum(gram.reshape(near, -1, LANES), 0).reshape(gram.shape)
    column_energy = jnp.log(jnp.diagonal(gram) / total_rows)
    elongation, raw = member_forces(snapshots, below, member_ends, member_dir, member_stiff)
    returned = shifted(raw[:, node_count:, :], "span", -1)
    upper, inverse, first, sums = first_pass(gram, flattened, elongation, member_stiff)
    sums = all_sum(sums.reshape(near, -1, LANES), 1).reshape(sums.shape)
    basis, forces, reduced, coef = second_pass(
        sums, upper, inverse, first, raw, returned, total_rows
    )
    return (basis.reshape(snapshots.shape), forces, reduced, coef, column_energy)


def solution(mesh):
    return jax.shard_map(
        local,
        mesh=mesh,
        in_specs=(
            P(None, SPAN_XSEC_LEAF, None),
            P(None, SPAN_XSEC_LEAF),
            P(None, SPAN_XSEC_LEAF),
            P(SPAN_XSEC_LEAF),
        ),
        out_specs=(P(None, SPAN_XSEC_LEAF, None), P(None, SPAN_XSEC_LEAF, None), P(), P(), P()),
        check_vma=False,
    )
```

```python
import functools
import math

import jax
import jax.numpy as jnp
from jax import lax
from jax.experimental import pallas as pl
from jax.experimental.pallas import tpu as pltpu
from jax.sharding import PartitionSpec as P

SEC_NODES = 128
SPAN_XSEC_LEAF = ("span", "xsec", "leaf")
TILE = 8
LANES = 128
CHUNK = 256

highest = lax.Precision.HIGHEST
f32 = jnp.float32


class DeviceSum:
    def __init__(self, part, arrived, planes, gathered, sent, got):
        self.part, self.arrived, self.planes, self.gathered = part, arrived, planes, gathered
        self.sent, self.got = sent, got
        self.near, self.far = part.shape[0], planes.shape[0]
        self.leaves = lax.axis_size("leaf")
        self.chips = self.near // (2 * self.leaves)
        self.span, self.xsec, self.leaf = (lax.axis_index(name) for name in SPAN_XSEC_LEAF)
        self.own = self.xsec * self.leaves + self.leaf

    def place(self, step):
        chip = (self.xsec // 2 + (step // 2) % self.chips) % self.chips
        side = (self.leaf + step // (2 * self.chips)) % self.leaves
        return chip * 2 + (self.xsec + step % 2) % 2, side

    def in_slab(self, step):
        other, side = self.place(step)
        return {"xsec": other, "leaf": side}

    def slab_above(self, step):
        return {"span": (self.span + step) % self.far}

    def scatter(self, step):
        other, side = self.place(step)
        return pltpu.make_async_remote_copy(
            self.part.at[other * self.leaves + side], self.arrived.at[step],
            self.sent.at[0, step], self.got.at[0, step], self.in_slab(step),
        )

    def exchange(self, step):
        block = self.planes.at[self.span]
        return pltpu.make_async_remote_copy(
            block, block, self.sent.at[1, step], self.got.at[1, step], self.slab_above(step)
        )

    def gather(self, step):
        block = self.gathered.at[self.own]
        return pltpu.make_async_remote_copy(
            block, block, self.sent.at[2, step], self.got.at[2, step], self.in_slab(step)
        )

    def each(self, count, act):
        lax.fori_loop(1, count, lambda step, _: (act(step), 0)[1], 0)

    def greet(self):
        barrier = pltpu.get_barrier_semaphore()
        signal = lambda where: pl.semaphore_signal(barrier, inc=1, device_id=where)
        self.each(self.near, lambda step: signal(self.in_slab(step)))
        self.each(self.far, lambda step: signal(self.slab_above(step)))

    def meet(self):
        pl.semaphore_wait(pltpu.get_barrier_semaphore(), self.near + self.far - 2)

    def start_scatter(self):
        self.each(self.near, lambda step: self.scatter(step).start())

    def start_exchange(self):
        self.each(self.near, lambda step: self.scatter(step).wait_recv())
        block = self.part[self.own]
        for step in range(1, self.near):
            block = block + self.arrived[step]
        self.planes[self.span] = block
        self.each(self.far, lambda step: self.exchange(step).start())

    def start_gather(self):
        self.each(self.far, lambda step: self.exchange(step).wait_recv())
        block = self.planes[0]
        for other in range(1, self.far):
            block = block + self.planes[other]
        self.gathered[self.own] = block
        self.each(self.near, lambda step: self.gather(step).start())

    def finish(self, total):
        self.each(self.near, lambda step: self.gather(step).wait_recv())
        lines = self.part.shape[1]
        for other in range(self.near):
            total[lines * other : lines * (other + 1), :] = self.gathered[other]
        self.each(self.near, lambda step: self.scatter(step).wait_send())
        self.each(self.far, lambda step: self.exchange(step).wait_send())
        self.each(self.near, lambda step: self.gather(step).wait_send())

    def take(self, flat):
        lines = self.part.shape[1]
        for other in range(self.near):
            self.part[other] = flat[lines * other : lines * (other + 1), :]


def sum_scratch(near, far, lines):
    blocks = pltpu.VMEM((near, lines, LANES), f32)
    pairs = pltpu.SemaphoreType.DMA((3, near))
    return [blocks, blocks, pltpu.VMEM((far, lines, LANES), f32), blocks, pairs, pairs]


def dot_f32(a, b, over_a=1, over_b=0):
    return lax.dot_general(
        a, b, (((over_a,), (over_b,)), ((), ())), precision=highest, preferred_element_type=f32
    )


def dot_bf16(a, b):
    return jnp.dot(a, b, preferred_element_type=f32)


def in_three(x):
    high = x.astype(jnp.bfloat16)
    rest = x - high.astype(f32)
    middle = rest.astype(jnp.bfloat16)
    return high, middle, (rest - middle.astype(f32)).astype(jnp.bfloat16)


def over_lanes(column):
    return jnp.broadcast_to(column, (TILE, LANES))


def over_rows(row):
    return jnp.broadcast_to(row, (TILE, LANES))


def factor_block(block):
    count = LANES // TILE
    lane = lax.broadcasted_iota(jnp.int32, (TILE, LANES), 1)
    sub = lax.broadcasted_iota(jnp.int32, (TILE, LANES), 0)
    left = [block[TILE * i : TILE * i + TILE, :] for i in range(count)]
    right = [jnp.where(lane == sub + TILE * i, 1.0, 0.0).astype(f32) for i in range(count)]
    for k in range(count):
        own_left, own_right = left[k], right[k]
        at = TILE * k
        columns = [over_lanes(own_left[:, at + j : at + j + 1]) for j in range(TILE)]
        pivot_left, pivot_right, pivot_columns, inverse = [], [], [], []
        scale = jnp.zeros((TILE, LANES), f32)
        for j in range(TILE):
            pivot = over_rows(columns[j][j : j + 1, :])
            inverse.append(1.0 / pivot)
            pivot_left.append(over_rows(own_left[j : j + 1, :]))
            pivot_right.append(over_rows(own_right[j : j + 1, :]))
            pivot_columns.append([over_rows(columns[l][j : j + 1, :]) for l in range(TILE)])
            factor = jnp.where(sub > j, columns[j] * inverse[j], 0.0)
            for l in range(j + 1, TILE):
                columns[l] = columns[l] - factor * pivot_columns[j][l]
            own_left = own_left - factor * pivot_left[j]
            own_right = own_right - factor * pivot_right[j]
            scale = jnp.where(sub == j, lax.rsqrt(pivot), scale)
        for i in range(k + 1, count):
            columns = [over_lanes(left[i][:, at + j : at + j + 1]) for j in range(TILE)]
            row_left, row_right = left[i], right[i]
            for j in range(TILE):
                factor = columns[j] * inverse[j]
                for l in range(j + 1, TILE):
                    columns[l] = columns[l] - factor * pivot_columns[j][l]
                row_left = row_left - factor * pivot_left[j]
                row_right = row_right - factor * pivot_right[j]
            left[i], right[i] = row_left, row_right
        left[k] = jnp.where(lane >= sub + at, own_left * scale, 0.0)
        right[k] = own_right * scale
    return jnp.concatenate(left, 0), jnp.concatenate(right, 0)


def factor_into(gram_ref, upper_ref, inverse_ref):
    upper_a, lower_a = factor_block(gram_ref[:LANES, :])
    across = dot_f32(lower_a, gram_ref[LANES : 2 * LANES, :])
    corner = gram_ref[2 * LANES : 3 * LANES, :] - dot_f32(across, across, 0, 0)
    upper_b, lower_b = factor_block(corner)
    zero = jnp.zeros((LANES, LANES), f32)
    upper_ref[:LANES, :LANES] = upper_a
    upper_ref[:LANES, LANES:] = across
    upper_ref[LANES:, :LANES] = zero
    upper_ref[LANES:, LANES:] = upper_b
    inverse_a, inverse_b = lower_a.T, lower_b.T
    inverse_ref[:LANES, :LANES] = inverse_a
    inverse_ref[:LANES, LANES:] = -dot_f32(inverse_a, dot_f32(across, inverse_b))
    inverse_ref[LANES:, :LANES] = zero
    inverse_ref[LANES:, LANES:] = inverse_b


def put_product(flat, start, a, b):
    top = dot_f32(a[:, :LANES], b, 0, 0)
    flat[start : start + LANES, :] = top[:, :LANES]
    flat[start + LANES : start + 2 * LANES, :] = top[:, LANES:]
    flat[start + 2 * LANES : start + 3 * LANES, :] = dot_f32(a[:, LANES:], b[:, LANES:], 0, 0)


def from_blocks(flat, start):
    across = flat[start + LANES : start + 2 * LANES, :]
    top = jnp.concatenate([flat[start : start + LANES, :], across], 1)
    low = jnp.concatenate([across.T, flat[start + 2 * LANES : start + 3 * LANES, :]], 1)
    return jnp.concatenate([top, low], 0)


def gram_and_members(
    field, ends, direction, stiff, gram, elongation, forces,
    pick, spread, parts, below, table, flat, halo_sent, halo_got, *for_sum,
):
    total = DeviceSum(*for_sum)
    total.greet()
    components, own, width = field.shape
    nodes = own + below.shape[1]
    members = ends.shape[1]
    kept = jnp.where(total.span == 0, own, nodes)

    def halo(c):
        return pltpu.make_async_remote_copy(
            field.at[c, 2 * own - nodes : own], below.at[c], halo_sent.at[c], halo_got.at[c],
            total.slab_above(1),
        )

    flattened = field[...].reshape(components * own, width)
    put_product(flat, 0, flattened, flattened)
    total.take(flat)
    table[...] = jnp.concatenate(
        [direction[...], stiff[...], ends[...].astype(f32), jnp.zeros((2, members), f32)], 0
    ).T
    chunks = [slice(start, start + CHUNK) for start in range(0, members, CHUNK)]

    def split(c, start, ref):
        for p, piece in enumerate(in_three(ref[c])):
            parts[p, c, start : start + ref.shape[1], :] = piece

    def stretch(rows, cut):
        result = jnp.zeros((CHUNK, width), f32)
        for c in range(components):
            difference = dot_bf16(pick[rows, cut], parts[2, c, cut, :])
            difference = difference + dot_bf16(pick[rows, cut], parts[1, c, cut, :])
            difference = difference + dot_bf16(pick[rows, cut], parts[0, c, cut, :])
            result = result + table[rows, c : c + 1] * difference
        return result

    for c in range(components):
        split(c, 0, field)
    for rows in chunks:
        node = lax.broadcasted_iota(jnp.int32, (CHUNK, nodes), 1)
        node = jnp.where(node < kept, node, -1).astype(f32)
        chosen = jnp.where(node == table[rows, 4:5], 1.0, 0.0)
        chosen = chosen - jnp.where(node == table[rows, 5:6], 1.0, 0.0)
        pick[rows, :] = chosen.astype(jnp.bfloat16)
        node = lax.broadcasted_iota(jnp.int32, (nodes, CHUNK), 0)
        node = jnp.where(node < kept, node, -1)
        chosen = jnp.where(node == ends[0:1, rows], 1.0, 0.0)
        chosen = chosen - jnp.where(node == ends[1:2, rows], 1.0, 0.0)
        spread[:, rows] = chosen.astype(jnp.bfloat16)
        elongation[rows, :] = stretch(rows, slice(0, own))
    total.meet()
    total.start_scatter()
    for c in range(components - 1):
        halo(c).start()
    total.start_exchange()
    halo(components - 1).start()
    for c in range(components):
        halo(c).wait_recv()
        split(c, own, below)
    total.start_gather()
    forces[...] = jnp.zeros_like(forces)
    for rows in chunks:
        whole = elongation[rows, :] + stretch(rows, slice(own, nodes))
        elongation[rows, :] = whole
        pull = whole * table[rows, 3:4]
        for c in range(components):
            high, middle, low = in_three(table[rows, c : c + 1] * pull)
            push = dot_bf16(spread[:, rows], low) + dot_bf16(spread[:, rows], middle)
            forces[c] = forces[c] + (push + dot_bf16(spread[:, rows], high))
    total.finish(gram)
    for c in range(components):
        halo(c).wait_send()


def first_stage(field, ends, direction, stiff):
    components, own, width = field.shape
    nodes, members = own + SEC_NODES, ends.shape[1]
    near, far = lax.axis_size("xsec") * lax.axis_size("leaf"), lax.axis_size("span")
    halo = pltpu.SemaphoreType.DMA((components,))
    return pl.pallas_call(
        gram_and_members,
        out_shape=(
            jax.ShapeDtypeStruct((3 * LANES, LANES), f32),
            jax.ShapeDtypeStruct((members, width), f32),
            jax.ShapeDtypeStruct((components, nodes, width), f32),
        ),
        scratch_shapes=[
            pltpu.VMEM((members, nodes), jnp.bfloat16),
            pltpu.VMEM((nodes, members), jnp.bfloat16),
            pltpu.VMEM((3, components, nodes, width), jnp.bfloat16),
            pltpu.VMEM((components, SEC_NODES, width), f32),
            pltpu.VMEM((members, TILE), f32),
            pltpu.VMEM((3 * LANES, LANES), f32),
            halo,
            halo,
            *sum_scratch(near, far, 3 * LANES // near),
        ],
        compiler_params=pltpu.CompilerParams(
            collective_id=0, has_side_effects=True, vmem_limit_bytes=60 << 20
        ),
        name="gram_and_members",
    )(field, ends, direction, stiff.reshape(1, -1))


def factor_and_sums(
    gram, field, elongation, stiff, raw, upper, inverse, first, sums, returned,
    landed, flat, halo_sent, halo_got, *for_sum,
):
    total = DeviceSum(*for_sum)
    total.greet()
    components, count, width = landed.shape
    own = raw.shape[1] - count

    def halo(c):
        return pltpu.make_async_remote_copy(
            raw.at[c, own : own + count], landed.at[c], halo_sent.at[c], halo_got.at[c],
            total.slab_above(total.far - 1),
        )

    factor_into(gram, upper, inverse)
    total.meet()
    for c in range(components):
        halo(c).start()
    transform = inverse[...]
    flattened = field[...].reshape(first.shape)
    first[...] = dot_f32(flattened, transform)
    put_product(flat, 0, first[...], first[...])
    stretch = dot_f32(elongation[...], transform)
    pull = stretch * jnp.broadcast_to(stiff[...], (TILE, stiff.shape[1])).T[:, :1]
    put_product(flat, 3 * LANES, stretch, pull)
    total.take(flat)
    total.start_scatter()
    total.start_exchange()
    for c in range(components):
        halo(c).wait_recv()
    returned[...] = landed[...]
    total.start_gather()
    total.finish(sums)
    for c in range(components):
        halo(c).wait_send()


def second_stage(gram, field, elongation, stiff, raw):
    components, own, width = field.shape
    square = jax.ShapeDtypeStruct((width, width), f32)
    near, far = lax.axis_size("xsec") * lax.axis_size("leaf"), lax.axis_size("span")
    halo = pltpu.SemaphoreType.DMA((components,))
    return pl.pallas_call(
        factor_and_sums,
        out_shape=(
            square,
            square,
            jax.ShapeDtypeStruct((components * own, width), f32),
            jax.ShapeDtypeStruct((6 * LANES, LANES), f32),
            jax.ShapeDtypeStruct((components, SEC_NODES, width), f32),
        ),
        scratch_shapes=[
            pltpu.VMEM((components, SEC_NODES, width), f32),
            pltpu.VMEM((6 * LANES, LANES), f32),
            halo,
            halo,
            *sum_scratch(near, far, 6 * LANES // near),
        ],
        compiler_params=pltpu.CompilerParams(
            collective_id=1, has_side_effects=True, vmem_limit_bytes=60 << 20
        ),
        name="factor_and_sums",
    )(gram, field, elongation, stiff.reshape(1, -1), raw)


def outputs_kernel(
    total_rows, gram, sums, upper_first, inverse_first, first, raw, returned,
    basis, forces, reduced, coef, energy, upper, inverse,
):
    components, own, width = forces.shape
    root = math.sqrt(total_rows)
    low = own - returned.shape[1]
    factor_into(sums, upper, inverse)
    transform = inverse[...]
    basis[...] = dot_f32(first[...], transform) * root
    both = dot_f32(inverse_first[...], transform) * root
    for c in range(components):
        forces[c, :low, :] = dot_f32(raw[c, :low, :], both)
        forces[c, low:, :] = dot_f32(raw[c, low:own, :] + returned[c], both)
    product = from_blocks(sums, 3 * LANES)
    reduced[...] = dot_f32(transform, dot_f32(product, transform), 0, 0)
    coef[...] = dot_f32(upper[...], upper_first[...]) * (1.0 / root)
    diagonal = lax.broadcasted_iota(jnp.int32, (LANES, LANES), 0)
    diagonal = diagonal == lax.broadcasted_iota(jnp.int32, (LANES, LANES), 1)
    for half, start in enumerate((0, 2 * LANES)):
        squares = jnp.sum(jnp.where(diagonal, gram[start : start + LANES, :], 0.0), 0, keepdims=True)
        energy[:, half * LANES : (half + 1) * LANES] = jnp.log(squares / total_rows)


def outputs(gram, sums, upper, inverse, first, raw, returned, total_rows):
    components, _, width = raw.shape
    own = first.shape[0] // components
    square = jax.ShapeDtypeStruct((width, width), f32)
    return pl.pallas_call(
        functools.partial(outputs_kernel, total_rows),
        out_shape=(
            jax.ShapeDtypeStruct(first.shape, f32),
            jax.ShapeDtypeStruct((components, own, width), f32),
            square,
            square,
            jax.ShapeDtypeStruct((1, width), f32),
        ),
        scratch_shapes=[pltpu.VMEM((width, width), f32)] * 2,
        compiler_params=pltpu.CompilerParams(vmem_limit_bytes=60 << 20),
        name="outputs",
    )(gram, sums, upper, inverse, first, raw, returned)


def local(snapshots, member_ends, member_dir, member_stiff):
    components, node_count, width = snapshots.shape
    devices_all = lax.axis_size(SPAN_XSEC_LEAF)
    total_rows = components * node_count * devices_all
    gram, elongation, raw = first_stage(snapshots, member_ends, member_dir, member_stiff)
    upper, inverse, first, sums, returned = second_stage(
        gram, snapshots, elongation, member_stiff, raw
    )
    basis, forces, reduced, coef, energy = outputs(
        gram, sums, upper, inverse, first, raw, returned, total_rows
    )
    return (basis.reshape(snapshots.shape), forces, reduced, coef, energy.reshape(width))


def solution(mesh):
    return jax.shard_map(
        local,
        mesh=mesh,
        in_specs=(
            P(None, SPAN_XSEC_LEAF, None),
            P(None, SPAN_XSEC_LEAF),
            P(None, SPAN_XSEC_LEAF),
            P(SPAN_XSEC_LEAF),
        ),
        out_specs=(P(None, SPAN_XSEC_LEAF, None), P(None, SPAN_XSEC_LEAF, None), P(), P(), P()),
        check_vma=False,
    )
```

```python
import functools
import math

import jax
import jax.numpy as jnp
from jax import lax
from jax.experimental import pallas as pl
from jax.experimental.pallas import tpu as pltpu
from jax.sharding import PartitionSpec as P

SEC_NODES = 128
SPAN_XSEC_LEAF = ("span", "xsec", "leaf")
TILE = 8
LANES = 128
CHUNK = 256

highest = lax.Precision.HIGHEST
f32 = jnp.float32


class DeviceSum:
    def __init__(self, part, arrived, planes, gathered, sent, got):
        self.part, self.arrived, self.planes, self.gathered = part, arrived, planes, gathered
        self.sent, self.got = sent, got
        self.near, self.far = part.shape[0], planes.shape[0]
        self.leaves = lax.axis_size("leaf")
        self.chips = self.near // (2 * self.leaves)
        self.span, self.xsec, self.leaf = (lax.axis_index(name) for name in SPAN_XSEC_LEAF)
        self.own = self.xsec * self.leaves + self.leaf
        self.chip, self.core = lax.div(self.xsec, 2), lax.rem(self.xsec, 2)
        around = lambda steps, length: min(steps, length - steps)
        hops = lambda step: around(step // 2 % self.chips, self.chips) + around(
            step // (2 * self.chips), self.leaves
        )
        self.slab_steps = sorted(range(1, self.near), key=lambda step: -hops(step))
        self.span_steps = sorted(range(1, self.far), key=lambda step: -around(step, self.far))

    def place(self, step):
        chip = lax.rem(self.chip + step // 2 % self.chips, self.chips)
        core = lax.rem(self.core + step % 2, 2)
        return chip * 2 + core, lax.rem(self.leaf + step // (2 * self.chips), self.leaves)

    def in_slab(self, step):
        other, side = self.place(step)
        return {"xsec": other, "leaf": side}

    def slab_above(self, step):
        return {"span": lax.rem(self.span + step, self.far)}

    def scatter(self, step):
        other, side = self.place(step)
        return pltpu.make_async_remote_copy(
            self.part.at[other * self.leaves + side], self.arrived.at[step],
            self.sent.at[0, step], self.got.at[0, step], self.in_slab(step),
        )

    def exchange(self, step):
        block = self.planes.at[self.span]
        return pltpu.make_async_remote_copy(
            block, block, self.sent.at[1, step], self.got.at[1, step], self.slab_above(step)
        )

    def gather(self, step):
        block = self.gathered.at[self.own]
        return pltpu.make_async_remote_copy(
            block, block, self.sent.at[2, step], self.got.at[2, step], self.in_slab(step)
        )

    def each(self, count, act):
        for step in self.slab_steps if count == self.near else self.span_steps:
            act(step)

    def greet(self):
        barrier = pltpu.get_barrier_semaphore()
        signal = lambda where: pl.semaphore_signal(barrier, inc=1, device_id=where)
        self.each(self.near, lambda step: signal(self.in_slab(step)))
        self.each(self.far, lambda step: signal(self.slab_above(step)))

    def meet(self):
        pl.semaphore_wait(pltpu.get_barrier_semaphore(), self.near + self.far - 2)

    def start_scatter(self):
        self.each(self.near, lambda step: self.scatter(step).start())

    def start_exchange(self):
        self.each(self.near, lambda step: self.scatter(step).wait_recv())
        block = self.part[self.own]
        for step in range(1, self.near):
            block = block + self.arrived[step]
        self.planes[self.span] = block
        self.each(self.far, lambda step: self.exchange(step).start())

    def start_gather(self):
        self.each(self.far, lambda step: self.exchange(step).wait_recv())
        block = self.planes[0]
        for other in range(1, self.far):
            block = block + self.planes[other]
        self.gathered[self.own] = block
        self.each(self.near, lambda step: self.gather(step).start())

    def finish(self, total):
        self.each(self.near, lambda step: self.gather(step).wait_recv())
        lines = self.part.shape[1]
        for other in range(self.near):
            total[lines * other : lines * (other + 1), :] = self.gathered[other]
        self.each(self.near, lambda step: self.scatter(step).wait_send())
        self.each(self.far, lambda step: self.exchange(step).wait_send())
        self.each(self.near, lambda step: self.gather(step).wait_send())

    def take(self, flat):
        lines = self.part.shape[1]
        for other in range(self.near):
            self.part[other] = flat[lines * other : lines * (other + 1), :]


def sum_scratch(near, far, lines):
    blocks = pltpu.VMEM((near, lines, LANES), f32)
    pairs = pltpu.SemaphoreType.DMA((3, near))
    return [blocks, blocks, pltpu.VMEM((far, lines, LANES), f32), blocks, pairs, pairs]


def dot_f32(a, b, over_a=1, over_b=0):
    return lax.dot_general(
        a, b, (((over_a,), (over_b,)), ((), ())), precision=highest, preferred_element_type=f32
    )


def in_two(x):
    high = x.astype(jnp.bfloat16)
    return high, (x - high.astype(f32)).astype(jnp.bfloat16)


def dot_split(a, b, over_a=1, over_b=0):
    (high_a, low_a), (high_b, low_b) = in_two(a), in_two(b)
    dims = (((over_a,), (over_b,)), ((), ()))
    one = lambda x, y: lax.dot_general(x, y, dims, preferred_element_type=f32)
    return one(high_a, low_b) + one(low_a, high_b) + one(high_a, high_b)


def dot_bf16(a, b):
    return jnp.dot(a, b, preferred_element_type=f32)


def in_three(x):
    high = x.astype(jnp.bfloat16)
    rest = x - high.astype(f32)
    middle = rest.astype(jnp.bfloat16)
    return high, middle, (rest - middle.astype(f32)).astype(jnp.bfloat16)


def over_lanes(column):
    return jnp.broadcast_to(column, (TILE, LANES))


def over_rows(row):
    return jnp.broadcast_to(row, (TILE, LANES))


def factor_block(block):
    count = LANES // TILE
    lane = lax.broadcasted_iota(jnp.int32, (TILE, LANES), 1)
    sub = lax.broadcasted_iota(jnp.int32, (TILE, LANES), 0)
    left = [block[TILE * i : TILE * i + TILE, :] for i in range(count)]
    right = [jnp.where(lane == sub + TILE * i, 1.0, 0.0).astype(f32) for i in range(count)]
    for k in range(count):
        own_left, own_right = left[k], right[k]
        at = TILE * k
        columns = [over_lanes(own_left[:, at + j : at + j + 1]) for j in range(TILE)]
        pivot_left, pivot_right, pivot_columns, inverse = [], [], [], []
        scale = jnp.zeros((TILE, LANES), f32)
        for j in range(TILE):
            pivot = over_rows(columns[j][j : j + 1, :])
            inverse.append(1.0 / pivot)
            pivot_left.append(over_rows(own_left[j : j + 1, :]))
            pivot_right.append(over_rows(own_right[j : j + 1, :]))
            pivot_columns.append([over_rows(columns[l][j : j + 1, :]) for l in range(TILE)])
            factor = jnp.where(sub > j, columns[j] * inverse[j], 0.0)
            for l in range(j + 1, TILE):
                columns[l] = columns[l] - factor * pivot_columns[j][l]
            own_left = own_left - factor * pivot_left[j]
            own_right = own_right - factor * pivot_right[j]
            scale = jnp.where(sub == j, lax.rsqrt(pivot), scale)
        for i in range(k + 1, count):
            columns = [over_lanes(left[i][:, at + j : at + j + 1]) for j in range(TILE)]
            row_left, row_right = left[i], right[i]
            for j in range(TILE):
                factor = columns[j] * inverse[j]
                for l in range(j + 1, TILE):
                    columns[l] = columns[l] - factor * pivot_columns[j][l]
                row_left = row_left - factor * pivot_left[j]
                row_right = row_right - factor * pivot_right[j]
            left[i], right[i] = row_left, row_right
        left[k] = jnp.where(lane >= sub + at, own_left * scale, 0.0)
        right[k] = own_right * scale
    return jnp.concatenate(left, 0), jnp.concatenate(right, 0)


def factor_into(gram_ref, upper_ref, inverse_ref):
    upper_a, lower_a = factor_block(gram_ref[:LANES, :])
    across = dot_f32(lower_a, gram_ref[LANES : 2 * LANES, :])
    corner = gram_ref[2 * LANES : 3 * LANES, :] - dot_f32(across, across, 0, 0)
    upper_b, lower_b = factor_block(corner)
    zero = jnp.zeros((LANES, LANES), f32)
    upper_ref[:LANES, :LANES] = upper_a
    upper_ref[:LANES, LANES:] = across
    upper_ref[LANES:, :LANES] = zero
    upper_ref[LANES:, LANES:] = upper_b
    inverse_a, inverse_b = lower_a.T, lower_b.T
    inverse_ref[:LANES, :LANES] = inverse_a
    inverse_ref[:LANES, LANES:] = -dot_f32(inverse_a, dot_f32(across, inverse_b))
    inverse_ref[LANES:, :LANES] = zero
    inverse_ref[LANES:, LANES:] = inverse_b


def put_product(flat, start, a, b, dot):
    top = dot(a[:, :LANES], b, 0, 0)
    flat[start : start + LANES, :] = top[:, :LANES]
    flat[start + LANES : start + 2 * LANES, :] = top[:, LANES:]
    flat[start + 2 * LANES : start + 3 * LANES, :] = dot(a[:, LANES:], b[:, LANES:], 0, 0)


def from_blocks(flat, start):
    across = flat[start + LANES : start + 2 * LANES, :]
    top = jnp.concatenate([flat[start : start + LANES, :], across], 1)
    low = jnp.concatenate([across.T, flat[start + 2 * LANES : start + 3 * LANES, :]], 1)
    return jnp.concatenate([top, low], 0)


def gram_and_members(
    field, ends, direction, stiff, gram, elongation_out, forces_out,
    elongation, forces, out_done, pick, spread, parts, below, table, flat, halo_sent, halo_got, *for_sum,
):
    total = DeviceSum(*for_sum)
    total.greet()
    components, own, width = field.shape
    nodes = own + below.shape[1]
    members = ends.shape[1]
    kept = jnp.where(total.span == 0, own, nodes)

    def halo(c):
        return pltpu.make_async_remote_copy(
            field.at[c, 2 * own - nodes : own], below.at[c], halo_sent.at[c], halo_got.at[c],
            total.slab_above(1),
        )

    flattened = field[...].reshape(components * own, width)
    put_product(flat, 0, flattened, flattened, dot_f32)
    total.take(flat)
    table[...] = jnp.concatenate(
        [direction[...], stiff[...], ends[...].astype(f32), jnp.zeros((2, members), f32)], 0
    ).T
    chunks = [slice(start, start + CHUNK) for start in range(0, members, CHUNK)]

    def split(c, start, ref):
        for p, piece in enumerate(in_three(ref[c])):
            parts[p, c, start : start + ref.shape[1], :] = piece

    def stretch(rows, cut, which, result):
        for c in which:
            difference = dot_bf16(pick[rows, cut], parts[2, c, cut, :])
            difference = difference + dot_bf16(pick[rows, cut], parts[1, c, cut, :])
            difference = difference + dot_bf16(pick[rows, cut], parts[0, c, cut, :])
            result = result + table[rows, c : c + 1] * difference
        return result

    for c in range(components):
        split(c, 0, field)
    for rows in chunks:
        node = lax.broadcasted_iota(jnp.int32, (CHUNK, nodes), 1)
        node = jnp.where(node < kept, node, -1).astype(f32)
        chosen = jnp.where(node == table[rows, 4:5], 1.0, 0.0)
        chosen = chosen - jnp.where(node == table[rows, 5:6], 1.0, 0.0)
        pick[rows, :] = chosen.astype(jnp.bfloat16)
        node = lax.broadcasted_iota(jnp.int32, (nodes, CHUNK), 0)
        node = jnp.where(node < kept, node, -1)
        chosen = jnp.where(node == ends[0:1, rows], 1.0, 0.0)
        chosen = chosen - jnp.where(node == ends[1:2, rows], 1.0, 0.0)
        spread[:, rows] = chosen.astype(jnp.bfloat16)
    total.meet()
    total.start_scatter()
    for c in range(components - 1):
        halo(c).start()
    for rows in chunks:
        zero = jnp.zeros((CHUNK, width), f32)
        elongation[rows, :] = stretch(rows, slice(0, own), range(components), zero)
    total.start_exchange()
    halo(components - 1).start()
    for c in range(components - 1):
        halo(c).wait_recv()
        split(c, own, below)
    for rows in chunks:
        elongation[rows, :] = stretch(
            rows, slice(own, nodes), range(components - 1), elongation[rows, :]
        )
    total.start_gather()
    halo(components - 1).wait_recv()
    split(components - 1, own, below)
    forces[...] = jnp.zeros_like(forces)
    for rows in chunks:
        whole = stretch(rows, slice(own, nodes), [components - 1], elongation[rows, :])
        elongation[rows, :] = whole
        pull = whole * table[rows, 3:4]
        for c in range(components):
            high, middle, low = in_three(table[rows, c : c + 1] * pull)
            push = dot_bf16(spread[:, rows], low) + dot_bf16(spread[:, rows], middle)
            forces[c] = forces[c] + (push + dot_bf16(spread[:, rows], high))
    leave = [
        pltpu.make_async_copy(elongation, elongation_out, out_done.at[0]),
        pltpu.make_async_copy(forces, forces_out, out_done.at[1]),
    ]
    for copy in leave:
        copy.start()
    total.finish(gram)
    for c in range(components):
        halo(c).wait_send()
    for copy in leave:
        copy.wait()


def first_stage(field, ends, direction, stiff):
    components, own, width = field.shape
    nodes, members = own + SEC_NODES, ends.shape[1]
    near, far = lax.axis_size("xsec") * lax.axis_size("leaf"), lax.axis_size("span")
    halo = pltpu.SemaphoreType.DMA((components,))
    return pl.pallas_call(
        gram_and_members,
        out_shape=(
            jax.ShapeDtypeStruct((3 * LANES, LANES), f32),
            jax.ShapeDtypeStruct((members, width), f32),
            jax.ShapeDtypeStruct((components, nodes, width), f32),
        ),
        out_specs=(
            pl.BlockSpec(memory_space=pltpu.VMEM),
            pl.BlockSpec(memory_space=pl.ANY),
            pl.BlockSpec(memory_space=pl.ANY),
        ),
        scratch_shapes=[
            pltpu.VMEM((members, width), f32),
            pltpu.VMEM((components, nodes, width), f32),
            pltpu.SemaphoreType.DMA((2,)),
            pltpu.VMEM((members, nodes), jnp.bfloat16),
            pltpu.VMEM((nodes, members), jnp.bfloat16),
            pltpu.VMEM((3, components, nodes, width), jnp.bfloat16),
            pltpu.VMEM((components, SEC_NODES, width), f32),
            pltpu.VMEM((members, TILE), f32),
            pltpu.VMEM((3 * LANES, LANES), f32),
            halo,
            halo,
            *sum_scratch(near, far, 3 * LANES // near),
        ],
        compiler_params=pltpu.CompilerParams(
            collective_id=0, has_side_effects=True, vmem_limit_bytes=60 << 20
        ),
        name="gram_and_members",
    )(field, ends, direction, stiff.reshape(1, -1))


def factor_and_sums(
    gram, field_in, elongation_in, stiff, raw_in, upper, first, forces, sums,
    inverse, field, elongation, raw, in_done, landed, flat, halo_sent, halo_got, *for_sum,
):
    total = DeviceSum(*for_sum)
    total.greet()
    components, count, width = landed.shape
    own = raw.shape[1] - count

    def halo(c):
        return pltpu.make_async_remote_copy(
            raw.at[c, own : own + count], landed.at[c], halo_sent.at[c], halo_got.at[c],
            total.slab_above(total.far - 1),
        )

    enter = [
        pltpu.make_async_copy(source, target, in_done.at[i])
        for i, (source, target) in enumerate(
            ((raw_in, raw), (field_in, field), (elongation_in, elongation))
        )
    ]
    for copy in enter:
        copy.start()
    factor_into(gram, upper, inverse)
    for copy in enter:
        copy.wait()
    total.meet()
    for c in range(components):
        halo(c).start()
    transform = inverse[...]
    flattened = field[...].reshape(first.shape)
    first[...] = dot_f32(flattened, transform)
    put_product(flat, 0, first[...], first[...], dot_split)
    stretch = dot_f32(elongation[...], transform)
    pull = stretch * jnp.broadcast_to(stiff[...], (TILE, stiff.shape[1])).T[:, :1]
    put_product(flat, 3 * LANES, stretch, pull, dot_split)
    total.take(flat)
    total.start_scatter()
    total.start_exchange()
    for c in range(components):
        halo(c).wait_recv()
        forces[c, : own - count, :] = dot_f32(raw[c, : own - count, :], transform)
        top = raw[c, own - count : own, :] + landed[c]
        forces[c, own - count :, :] = dot_f32(top, transform)
    total.start_gather()
    total.finish(sums)
    for c in range(components):
        halo(c).wait_send()


def second_stage(gram, field, elongation, stiff, raw):
    components, own, width = field.shape
    square = jax.ShapeDtypeStruct((width, width), f32)
    near, far = lax.axis_size("xsec") * lax.axis_size("leaf"), lax.axis_size("span")
    halo = pltpu.SemaphoreType.DMA((components,))
    return pl.pallas_call(
        factor_and_sums,
        out_shape=(
            square,
            jax.ShapeDtypeStruct((components * own, width), f32),
            jax.ShapeDtypeStruct((components, own, width), f32),
            jax.ShapeDtypeStruct((6 * LANES, LANES), f32),
        ),
        in_specs=[
            pl.BlockSpec(memory_space=space)
            for space in (pltpu.VMEM, pl.ANY, pl.ANY, pltpu.VMEM, pl.ANY)
        ],
        scratch_shapes=[
            pltpu.VMEM((width, width), f32),
            pltpu.VMEM(field.shape, f32),
            pltpu.VMEM(elongation.shape, f32),
            pltpu.VMEM(raw.shape, f32),
            pltpu.SemaphoreType.DMA((3,)),
            pltpu.VMEM((components, SEC_NODES, width), f32),
            pltpu.VMEM((6 * LANES, LANES), f32),
            halo,
            halo,
            *sum_scratch(near, far, 6 * LANES // near),
        ],
        compiler_params=pltpu.CompilerParams(
            collective_id=1, has_side_effects=True, vmem_limit_bytes=60 << 20
        ),
        name="factor_and_sums",
    )(gram, field, elongation, stiff.reshape(1, -1), raw)


def refine(gap, rounds):
    row = lax.broadcasted_iota(jnp.int32, gap.shape, 0)
    column = lax.broadcasted_iota(jnp.int32, gap.shape, 1)
    share = jnp.where(row < column, 1.0, jnp.where(row == column, 0.5, 0.0))
    change = None
    for last in [False] * (rounds - 1) + [True]:
        half = gap * share
        change = -half if change is None else change - half - dot_split(change, half)
        if not last:
            image = dot_split(gap, half)
            gap = dot_split(half, half + image, 0, 0) - (image + image.T)
    return change, gap


def outputs_kernel(
    total_rows, gram, sums, upper_first, first, forces_first,
    basis, forces, reduced, coef, energy, upper, inverse, change, growth,
):
    components, own, width = forces.shape
    root = math.sqrt(total_rows)
    row = lax.broadcasted_iota(jnp.int32, (width, width), 0)
    column = lax.broadcasted_iota(jnp.int32, (width, width), 1)
    identity = jnp.where(row == column, 1.0, 0.0)
    start = from_blocks(sums, 0) - identity
    step, gap = refine(start, 2)
    change[...] = step
    whole = start + step.T + dot_split(step, start, 0, 0)
    growth[...] = jnp.where(row <= column, whole, 0.0)

    @pl.when(jnp.logical_not(jnp.sum(gap * gap) < 1e-4))
    def _():
        factor_into(sums, upper, inverse)
        change[...] = inverse[...] - identity
        growth[...] = upper[...] - identity

    step = change[...]
    basis[...] = (first[...] + dot_split(first[...], step)) * root
    for c in range(components):
        forces[c] = (forces_first[c] + dot_split(forces_first[c], step)) * root
    product = from_blocks(sums, 3 * LANES)
    product = product + dot_split(product, step)
    reduced[...] = product + dot_split(step, product, 0, 0)
    coef[...] = (upper_first[...] + dot_split(growth[...], upper_first[...])) * (1.0 / root)
    diagonal = lax.broadcasted_iota(jnp.int32, (LANES, LANES), 0)
    diagonal = diagonal == lax.broadcasted_iota(jnp.int32, (LANES, LANES), 1)
    for half, start in enumerate((0, 2 * LANES)):
        squares = jnp.sum(jnp.where(diagonal, gram[start : start + LANES, :], 0.0), 0, keepdims=True)
        energy[:, half * LANES : (half + 1) * LANES] = jnp.log(squares / total_rows)


def outputs(gram, sums, upper, first, forces, total_rows):
    width = forces.shape[2]
    square = jax.ShapeDtypeStruct((width, width), f32)
    return pl.pallas_call(
        functools.partial(outputs_kernel, total_rows),
        out_shape=(
            jax.ShapeDtypeStruct(first.shape, f32),
            jax.ShapeDtypeStruct(forces.shape, f32),
            square,
            square,
            jax.ShapeDtypeStruct((1, width), f32),
        ),
        scratch_shapes=[pltpu.VMEM((width, width), f32)] * 4,
        compiler_params=pltpu.CompilerParams(vmem_limit_bytes=60 << 20),
        name="outputs",
    )(gram, sums, upper, first, forces)


def local(snapshots, member_ends, member_dir, member_stiff):
    components, node_count, width = snapshots.shape
    total_rows = components * node_count * lax.axis_size(SPAN_XSEC_LEAF)
    gram, elongation, raw = first_stage(snapshots, member_ends, member_dir, member_stiff)
    upper, first, forces, sums = second_stage(gram, snapshots, elongation, member_stiff, raw)
    basis, forces, reduced, coef, energy = outputs(gram, sums, upper, first, forces, total_rows)
    return (basis.reshape(snapshots.shape), forces, reduced, coef, energy.reshape(width))


def solution(mesh):
    return jax.shard_map(
        local,
        mesh=mesh,
        in_specs=(
            P(None, SPAN_XSEC_LEAF, None),
            P(None, SPAN_XSEC_LEAF),
            P(None, SPAN_XSEC_LEAF),
            P(SPAN_XSEC_LEAF),
        ),
        out_specs=(P(None, SPAN_XSEC_LEAF, None), P(None, SPAN_XSEC_LEAF, None), P(), P(), P()),
        check_vma=False,
    )
```
